32 devices in a mesh: seq: 8 (over z, x), head: 4 (over y, core).
Axes of the slice: x: 2, y: 2, z: 4, core: 2. Of those that a mesh axis runs over, the one named last changes fastest.
Arguments:
- queries: bfloat16 [1024, 1024], P('seq', 'head'), may hold values from -6 to 6
- keys: bfloat16 [1024, 1024], P('seq', 'head'), may hold values from -6 to 6
- values: bfloat16 [1024, 1024], P('seq', 'head'), may hold values from -3 to 3
- out_grad: bfloat16 [1024, 1024], P('seq', 'head'), may hold values from -3 to 3
- w_query: bfloat16 [1024, 2048], P('head'), may hold values from -0.1875 to 0.1875
- w_key: bfloat16 [1024, 2048], P('head'), may hold values from -0.1875 to 0.1875
- w_value: bfloat16 [1024, 2048], P('head'), may hold values from -0.1875 to 0.1875
Outputs:
- input_grad: bfloat16 [1024, 2048], P('seq', 'head')
The draws below stay inside these ranges and needn't reach their ends.
All inputs are finite; a program needn't handle non-finite values.
Results may differ from the reference program's by a relative error of at most 0.0064.
Values sent between devices are 32-bit elements; how exact they have to be, the bound alone decides.
A program may use at most 128 MiB of HBM per device.

```python
import jax
import jax.numpy as jnp
import numpy as np
from jax import lax

HD = 64
HEADS = 16
D = 2048
FEATS = 2080
TOK_DEV = 128
TOKENS = 1024
N_SEQ = 8


def block_scale(own_key, dims, shards, low, top_value):
    def one(dim, parts):
        heights = jax.random.uniform(jax.random.fold_in(jax.random.fold_in(own_key, 6), dim), (parts,), jnp.float32, low / len(shards), top_value / len(shards))
        return jnp.repeat(jnp.exp(heights), dims[dim] // parts).reshape((-1,) + (1,) * (len(dims) - dim - 1))

    loudness = one(*shards[0])
    for cut in shards[1:]:
        loudness = loudness * one(*cut)
    return loudness


def gaussian(own_key, extent, spread, reach, shards=(), kind=jnp.bfloat16):
    values = spread * jax.random.normal(own_key, extent, jnp.float32)
    if shards:
        values = values * block_scale(own_key, extent, shards, -0.22, 0.18)
    return jnp.clip(values, -reach, reach).astype(kind)


def setup_inputs(seed: int = 0) -> dict:
    seeds = jax.random.split(jax.random.key(seed), 8)
    queries = gaussian(seeds[0], (TOKENS, HEADS * HD), 1.0, 6.0, ((0, 8), (1, 4)))
    keys = gaussian(seeds[1], (TOKENS, HEADS * HD), 1.0, 6.0, ((0, 8), (1, 4)))
    values = gaussian(seeds[2], (TOKENS, HEADS * HD), 0.5, 3.0, ((0, 8), (1, 4)))
    out_grad = gaussian(seeds[3], (TOKENS, HEADS * HD), 0.5, 3.0, ((0, 8), (1, 4)))
    w_query = gaussian(seeds[4], (HEADS * HD, D), (HEADS * HD) ** -0.5, 0.1875, ((0, 4),))
    w_key = gaussian(seeds[5], (HEADS * HD, D), (HEADS * HD) ** -0.5, 0.1875, ((0, 4),))
    w_value = gaussian(seeds[6], (HEADS * HD, D), (HEADS * HD) ** -0.5, 0.1875, ((0, 4),))
    return {"queries": queries, "keys": keys, "values": values, "out_grad": out_grad, "w_query": w_query, "w_key": w_key, "w_value": w_value}


def pair_tables(width):
    first, second = np.triu_indices(width)
    count = first.shape[0]
    select_first = np.zeros((width, count), np.float32)
    select_second = np.zeros((width, count), np.float32)
    select_first[first, np.arange(count)] = 1.0
    select_second[second, np.arange(count)] = 1.0
    scaling = np.where(first == second, 1.0, np.sqrt(2.0)) / width
    return (select_first, select_second, scaling.astype(np.float32))

def expand_features(inputs, pick_first, pick_second, scaling):
    first = jnp.dot(inputs, pick_first, preferred_element_type=jnp.float32)
    second = jnp.dot(inputs, pick_second, preferred_element_type=jnp.float32)
    return (first.astype(jnp.bfloat16), second.astype(jnp.bfloat16), (first * second * scaling).astype(jnp.bfloat16))

def chain_back(first, second, dphi, back_first, back_second, scaling):
    left = dphi * scaling * second.astype(jnp.float32)
    right = dphi * scaling * first.astype(jnp.float32)
    return jnp.dot(left, back_first, precision=lax.Precision.HIGHEST, preferred_element_type=jnp.float32) + jnp.dot(right, back_second, precision=lax.Precision.HIGHEST, preferred_element_type=jnp.float32)

def reference(queries, keys, values, out_grad, w_query, w_key, w_value):
    select_first, select_second, scale_np = pair_tables(HD)
    pick_first = jnp.asarray(select_first, jnp.bfloat16)
    pick_second = jnp.asarray(select_second, jnp.bfloat16)
    back_first = jnp.asarray(select_first.T, jnp.float32)
    back_second = jnp.asarray(select_second.T, jnp.float32)
    scaling = jnp.asarray(scale_np, jnp.float32)

    def shaped(array):
        return array.reshape(N_SEQ, TOK_DEV, HEADS, HD)
    blocks = (shaped(queries), shaped(keys), shaped(values), shaped(out_grad))
    zero_state = jnp.zeros((FEATS, HEADS, HD), jnp.float32)

    def features_of(array):
        first, second, feats = expand_features(array.reshape(TOK_DEV * HEADS, HD), pick_first, pick_second, scaling)
        return (first, second, feats)

    def state_of(feats, other):
        return jnp.einsum('thf,thd->fhd', feats.reshape(TOK_DEV, HEADS, FEATS).astype(jnp.float32), other.astype(jnp.float32))

    def total_step(total, block):
        query_b, key_b, value_b, grad_b = block
        feats = features_of(query_b)[2]
        return (total + state_of(feats, grad_b), None)
    grad_total, unused = lax.scan(total_step, zero_state, blocks)
    causal = lax.broadcasted_iota(jnp.int32, (TOK_DEV, TOK_DEV), 0) >= lax.broadcasted_iota(jnp.int32, (TOK_DEV, TOK_DEV), 1)

    def step(carry, block):
        kv_sum, grad_sum = carry
        query_b, key_b, value_b, grad_b = block
        qfirst, qsecond, fq = features_of(query_b)
        kfirst, ksecond, fk = features_of(key_b)
        kv_local = state_of(fk, value_b)
        grad_local = state_of(fq, grad_b)
        kv_before = kv_sum.astype(jnp.bfloat16).astype(jnp.float32)
        grad_after = (grad_total - grad_sum - grad_local).astype(jnp.bfloat16).astype(jnp.float32)
        qf = query_b.astype(jnp.float32)
        kf = key_b.astype(jnp.float32)
        vf = value_b.astype(jnp.float32)
        gf = grad_b.astype(jnp.float32)
        scores = jnp.einsum('thd,shd->hts', qf, kf)
        products = jnp.einsum('thd,shd->hts', gf, vf)
        attn = jnp.where(causal, (scores / HD) ** 2, 0.0).astype(jnp.bfloat16).astype(jnp.float32)
        pgrad = jnp.where(causal, 2.0 * scores * products / (HD * HD), 0.0).astype(jnp.bfloat16).astype(jnp.float32)
        dfq = jnp.einsum('thd,fhd->thf', gf, kv_before).reshape(TOK_DEV * HEADS, FEATS)
        dfk = jnp.einsum('thd,fhd->thf', vf, grad_after).reshape(TOK_DEV * HEADS, FEATS)
        query_grad = jnp.einsum('hts,shd->thd', pgrad, kf) + chain_back(qfirst, qsecond, dfq, back_first, back_second, scaling).reshape(TOK_DEV, HEADS, HD)
        key_grad = jnp.einsum('hts,thd->shd', pgrad, qf) + chain_back(kfirst, ksecond, dfk, back_first, back_second, scaling).reshape(TOK_DEV, HEADS, HD)
        value_grad = jnp.einsum('hts,thd->shd', attn, gf) + jnp.einsum('thf,fhd->thd', fk.reshape(TOK_DEV, HEADS, FEATS).astype(jnp.float32), grad_after)
        mixed = jnp.dot(query_grad.astype(jnp.bfloat16).reshape(TOK_DEV, HEADS * HD), w_query, preferred_element_type=jnp.float32)
        mixed = mixed + jnp.dot(key_grad.astype(jnp.bfloat16).reshape(TOK_DEV, HEADS * HD), w_key, preferred_element_type=jnp.float32)
        mixed = mixed + jnp.dot(value_grad.astype(jnp.bfloat16).reshape(TOK_DEV, HEADS * HD), w_value, preferred_element_type=jnp.float32)
        return ((kv_sum + kv_local, grad_sum + grad_local), mixed.astype(jnp.bfloat16))
    unused_carry, result = lax.scan(step, (zero_state, zero_state), blocks)
    return result.reshape(N_SEQ * TOK_DEV, D)
```

```python
import functools

import jax
import jax.numpy as jnp
import numpy as np
from jax import lax
from jax.experimental import pallas as pl
from jax.experimental.pallas import tpu as pltpu
from jax.sharding import PartitionSpec as P

HD = 64
MESH = pl.DeviceIdType.MESH


def shifted(value, axis, steps):
    count = lax.axis_size(axis)
    leading, last = (max(0, -steps), min(count, count - steps))
    return lax.ppermute(value, axis, [(source, source + steps) for source in range(leading, last)])


def pair_tables(width):
    first, second = np.triu_indices(width)
    count = first.shape[0]
    select_first = np.zeros((width, count), np.float32)
    select_second = np.zeros((width, count), np.float32)
    select_first[first, np.arange(count)] = 1.0
    select_second[second, np.arange(count)] = 1.0
    scaling = np.where(first == second, 1.0, np.sqrt(2.0)) / width
    return (select_first, select_second, scaling.astype(np.float32))


def expand_features(inputs, pick_first, pick_second, scaling):
    first = jnp.dot(inputs, pick_first, preferred_element_type=jnp.bfloat16)
    second = jnp.dot(inputs, pick_second, preferred_element_type=jnp.bfloat16)
    feats = (first.astype(jnp.float32) * second.astype(jnp.float32) * scaling).astype(jnp.bfloat16)
    return (first, second, feats)


def chain_back(first, second, dphi, back_first, back_second, scaling):
    scaled = dphi * scaling
    left = scaled * second.astype(jnp.float32)
    right = scaled * first.astype(jnp.float32)
    return jnp.dot(
        left, back_first, precision=lax.Precision.HIGHEST, preferred_element_type=jnp.float32
    ) + jnp.dot(
        right, back_second, precision=lax.Precision.HIGHEST, preferred_element_type=jnp.float32
    )


def on_device(queries, keys, values, out_grad, w_query, w_key, w_value):
    count_rows = queries.shape[0]
    head_count = queries.shape[1] // HD
    select_first, select_second, scale_np = pair_tables(HD)
    pick_first = jnp.asarray(select_first, jnp.bfloat16)
    pick_second = jnp.asarray(select_second, jnp.bfloat16)
    back_first = jnp.asarray(select_first.T, jnp.float32)
    back_second = jnp.asarray(select_second.T, jnp.float32)
    scaling = jnp.asarray(scale_np, jnp.float32)
    feat_count = scale_np.shape[0]
    query_heads = queries.reshape(count_rows, head_count, HD)
    key_heads = keys.reshape(count_rows, head_count, HD)
    value_heads = values.reshape(count_rows, head_count, HD)
    grad_heads = out_grad.reshape(count_rows, head_count, HD)
    query_expanded = []
    key_expanded = []
    kv_parts = []
    grad_parts = []
    for number in range(head_count):
        query_set = expand_features(query_heads[:, number], pick_first, pick_second, scaling)
        key_set = expand_features(key_heads[:, number], pick_first, pick_second, scaling)
        query_expanded.append(query_set)
        key_expanded.append(key_set)
        kv_parts.append(
            jnp.einsum(
                "tf,td->fd", key_set[2], value_heads[:, number], preferred_element_type=jnp.float32
            )
        )
        grad_parts.append(
            jnp.einsum(
                "tf,td->fd", query_set[2], grad_heads[:, number], preferred_element_type=jnp.float32
            )
        )
    kv_local = jnp.stack(kv_parts, 1).reshape(feat_count, head_count * HD)
    grad_local = jnp.stack(grad_parts, 1).reshape(feat_count, head_count * HD)
    rounds = (lax.axis_size("seq") - 1).bit_length()
    kv_running = kv_local
    grad_running = grad_local
    for level in range(rounds):
        kv_running = kv_running + shifted(kv_running, "seq", 1 << level)
        grad_running = grad_running + shifted(grad_running, "seq", -(1 << level))
    kv_before = kv_running - kv_local
    grad_after = grad_running - grad_local
    kv_before = kv_before.astype(jnp.bfloat16).reshape(feat_count, head_count, HD)
    grad_after = grad_after.astype(jnp.bfloat16).reshape(feat_count, head_count, HD)
    causal = lax.broadcasted_iota(jnp.int32, (count_rows, count_rows), 0) >= lax.broadcasted_iota(
        jnp.int32, (count_rows, count_rows), 1
    )
    scores = jnp.einsum("thd,shd->hts", query_heads, key_heads, preferred_element_type=jnp.float32)
    products = jnp.einsum(
        "thd,shd->hts", grad_heads, value_heads, preferred_element_type=jnp.float32
    )
    attn = jnp.where(causal, (scores / HD) ** 2, 0.0).astype(jnp.bfloat16)
    pgrad = jnp.where(causal, 2.0 * scores * products / (HD * HD), 0.0).astype(jnp.bfloat16)
    query_local = jnp.einsum("hts,shd->thd", pgrad, key_heads, preferred_element_type=jnp.float32)
    key_local = jnp.einsum("hts,thd->shd", pgrad, query_heads, preferred_element_type=jnp.float32)
    value_local = jnp.einsum("hts,thd->shd", attn, grad_heads, preferred_element_type=jnp.float32)
    query_out = []
    key_out = []
    value_out = []
    for number in range(head_count):
        qfirst, qsecond, query_feat = query_expanded[number]
        kfirst, ksecond, key_feat = key_expanded[number]
        dfq = jnp.einsum(
            "td,fd->tf",
            grad_heads[:, number],
            kv_before[:, number],
            preferred_element_type=jnp.float32,
        )
        dfk = jnp.einsum(
            "td,fd->tf",
            value_heads[:, number],
            grad_after[:, number],
            preferred_element_type=jnp.float32,
        )
        query_out.append(
            query_local[:, number]
            + chain_back(qfirst, qsecond, dfq, back_first, back_second, scaling)
        )
        key_out.append(
            key_local[:, number]
            + chain_back(kfirst, ksecond, dfk, back_first, back_second, scaling)
        )
        value_out.append(
            value_local[:, number]
            + jnp.einsum(
                "tf,fd->td", key_feat, grad_after[:, number], preferred_element_type=jnp.float32
            )
        )
    query_grad = jnp.stack(query_out, 1).astype(jnp.bfloat16).reshape(count_rows, head_count * HD)
    key_grad = jnp.stack(key_out, 1).astype(jnp.bfloat16).reshape(count_rows, head_count * HD)
    value_grad = jnp.stack(value_out, 1).astype(jnp.bfloat16).reshape(count_rows, head_count * HD)
    partial_sum = jnp.dot(query_grad, w_query, preferred_element_type=jnp.float32)
    partial_sum = partial_sum + jnp.dot(key_grad, w_key, preferred_element_type=jnp.float32)
    partial_sum = partial_sum + jnp.dot(value_grad, w_value, preferred_element_type=jnp.float32)
    return lax.psum_scatter(partial_sum, "head", scatter_dimension=1, tiled=True).astype(
        jnp.bfloat16
    )


def stacked(block):
    lanes = lax.broadcasted_iota(jnp.int32, block.shape, 1)
    low = jnp.where(lanes < HD, block, 0.0).astype(jnp.bfloat16)
    high = jnp.where(lanes >= HD, block, 0.0).astype(jnp.bfloat16)
    return jnp.concatenate([low, high], axis=0)


def rows_dot(left, right):
    return lax.dot_general(
        left, right, (((1,), (1,)), ((), ())), preferred_element_type=jnp.float32
    )


def direct_kernel(
    n_seq,
    queries,
    keys,
    values,
    grads,
    wq_hbm,
    wk_hbm,
    wv_hbm,
    out,
    buffers,
    weights,
    totals,
    own_part,
    core_send,
    core_recv,
    far_send,
    far_recv,
    recv_sem,
    line_sem,
    side_sem,
    weight_sem,
    reduce_send_sem,
    reduce_recv_sem,
):
    K, V, Q, G = range(4)
    rows, width = queries.shape
    lines = n_seq // 2
    me = lax.axis_index("seq")
    line, side = me // 2, me % 2
    other = 2 * line + (1 - side)
    head = lax.axis_index("head")
    far, core = head // 2, head % 2
    core_mate = 2 * far + (1 - core)
    far_mate = 2 * (1 - far) + core
    out_width = out.shape[1]

    weight_copies = [
        pltpu.make_async_copy(source, weights.at[i], weight_sem.at[i])
        for i, source in enumerate((wq_hbm, wk_hbm, wv_hbm))
    ]
    for copy in weight_copies:
        copy.start()

    for which, ref in ((K, keys), (V, values), (Q, queries), (G, grads)):
        buffers[which, me] = ref[...].astype(jnp.float32)

    barrier = pltpu.get_barrier_semaphore()

    def greet(target):
        pl.semaphore_signal(barrier, inc=1, device_id=target, device_id_type=MESH)

    greet({"seq": other})
    greet({"head": core_mate})
    greet({"head": far_mate})
    has_up = line < lines - 1
    has_down = line > 0

    @pl.when(has_up)
    def _():
        greet({"seq": me + 2})

    @pl.when(has_down)
    def _():
        greet({"seq": me - 2})

    pl.semaphore_wait(barrier, 3 + has_up.astype(jnp.int32) + has_down.astype(jnp.int32))

    def transfer(which, block, sem, target):
        return pltpu.make_async_remote_copy(
            src_ref=buffers.at[which, block],
            dst_ref=buffers.at[which, block],
            send_sem=sem.at[which, block],
            recv_sem=recv_sem.at[which, block],
            device_id={"seq": target},
            device_id_type=MESH,
        )

    def along(which, block):
        return transfer(which, block, line_sem, me + 2 if which in (K, V) else me - 2)

    def across(which, block):
        return transfer(which, block, side_sem, other)

    def each_send(step, act):
        for pair in ((K, Q), (V, G)):
            for which in pair:
                rising = which in (K, V)
                block = me - 2 * step if rising else me + 2 * step
                present = (line >= step) if rising else (line + step < lines)
                onward = has_up if rising else has_down

                def body(which=which, block=block, rising=rising, onward=onward):
                    if step and act == "start":
                        along(which, block).wait_recv()

                    @pl.when(onward)
                    def _():
                        copy = along(which, block)
                        copy.start() if act == "start" else copy.wait_send()

                    def cross():
                        copy = across(which, block)
                        copy.start() if act == "start" else copy.wait_send()

                    if step:
                        cross()
                    else:
                        pl.when(side == (0 if rising else 1))(cross)

                if step:
                    pl.when(present)(body)
                else:
                    body()

    def query_role(block, diagonal=False):
        for cols in range(0, width, 2 * HD):
            part = slice(cols, cols + 2 * HD)
            k2 = stacked(buffers[K, block, :, part])
            v2 = stacked(buffers[V, block, :, part])
            scores = rows_dot(queries[:, part], k2)
            products = rows_dot(grads[:, part], v2)
            weight = scores * products * (2.0 / (HD * HD))
            if diagonal:
                t = lax.broadcasted_iota(jnp.int32, weight.shape, 0)
                s = lax.broadcasted_iota(jnp.int32, weight.shape, 1) % rows
                weight = jnp.where(t >= s, weight, 0.0)
            result = jnp.dot(
                weight.astype(jnp.bfloat16), k2, preferred_element_type=jnp.float32
            )
            if diagonal:
                totals[0, :, part] = result
            else:
                totals[0, :, part] += result

    def key_role(block, diagonal=False):
        for cols in range(0, width, 2 * HD):
            part = slice(cols, cols + 2 * HD)
            q2 = stacked(buffers[Q, block, :, part])
            g2 = stacked(buffers[G, block, :, part])
            scores = rows_dot(keys[:, part], q2)
            products = rows_dot(values[:, part], g2)
            weight = scores * products * (2.0 / (HD * HD))
            attn = (scores * (1.0 / HD)) * (scores * (1.0 / HD))
            if diagonal:
                s = lax.broadcasted_iota(jnp.int32, weight.shape, 0)
                t = lax.broadcasted_iota(jnp.int32, weight.shape, 1) % rows
                weight = jnp.where(t >= s, weight, 0.0)
                attn = jnp.where(t >= s, attn, 0.0)
            key_result = jnp.dot(
                weight.astype(jnp.bfloat16), q2, preferred_element_type=jnp.float32
            )
            value_result = jnp.dot(
                attn.astype(jnp.bfloat16), g2, preferred_element_type=jnp.float32
            )
            if diagonal:
                totals[1, :, part] = key_result
                totals[2, :, part] = value_result
            else:
                totals[1, :, part] += key_result
                totals[2, :, part] += value_result

    def crossed(step):
        kv_block = other - 2 * step
        qg_block = other + 2 * step

        def take_kv():
            across(K, kv_block).wait_recv()
            across(V, kv_block).wait_recv()
            query_role(kv_block)

        def take_qg():
            across(Q, qg_block).wait_recv()
            across(G, qg_block).wait_recv()
            key_role(qg_block)

        if step:
            pl.when(line >= step)(take_kv)
            pl.when(line + step < lines)(take_qg)
        else:
            pl.when(side == 1)(take_kv)
            pl.when(side == 0)(take_qg)

    each_send(0, "start")
    query_role(me, diagonal=True)
    key_role(me, diagonal=True)
    for step in range(1, lines):
        each_send(step, "start")

        @pl.when(line >= step)
        def _():
            query_role(me - 2 * step)

        @pl.when(line + step < lines)
        def _():
            key_role(me + 2 * step)

        crossed(step - 1)
    crossed(lines - 1)

    for copy in weight_copies:
        copy.wait()
    final = [totals[i].astype(jnp.bfloat16) for i in range(3)]

    def project(target):
        cols = pl.ds(pl.multiple_of(target * out_width, out_width), out_width)
        return sum(
            jnp.dot(final[i], weights[i, :, cols], preferred_element_type=jnp.float32)
            for i in range(3)
        )

    def to_core(slot):
        return pltpu.make_async_remote_copy(
            src_ref=core_send.at[slot],
            dst_ref=core_recv.at[slot],
            send_sem=reduce_send_sem.at[slot],
            recv_sem=reduce_recv_sem.at[slot],
            device_id={"head": core_mate},
            device_id_type=MESH,
        )

    to_far = pltpu.make_async_remote_copy(
        src_ref=far_send,
        dst_ref=far_recv,
        send_sem=reduce_send_sem.at[2],
        recv_sem=reduce_recv_sem.at[2],
        device_id={"head": far_mate},
        device_id_type=MESH,
    )
    core_send[0] = project(2 * (1 - far) + (1 - core))
    to_core(0).start()
    far_send[...] = project(far_mate)
    core_send[1] = project(core_mate)
    to_core(0).wait_recv()
    far_send[...] += core_recv[0]
    to_far.start()
    to_core(1).start()
    own_part[...] = project(head)
    to_core(1).wait_recv()
    own_part[...] += core_recv[1]
    to_far.wait_recv()
    out[...] = (own_part[...] + far_recv[...]).astype(out.dtype)

    to_core(0).wait_send()
    to_core(1).wait_send()
    to_far.wait_send()
    for step in range(lines):
        each_send(step, "finish")


def direct_form(n_seq, n_head, queries, keys, values, out_grad, w_query, w_key, w_value):
    rows, width = queries.shape
    model = w_query.shape[1]
    out_width = model // n_head
    vmem = pl.BlockSpec(memory_space=pltpu.VMEM)
    hbm = pl.BlockSpec(memory_space=pl.ANY)
    piece = (rows, out_width)
    return pl.pallas_call(
        functools.partial(direct_kernel, n_seq),
        out_shape=jax.ShapeDtypeStruct(piece, jnp.bfloat16),
        in_specs=[vmem] * 4 + [hbm] * 3,
        out_specs=vmem,
        scratch_shapes=[
            pltpu.VMEM((4, n_seq, rows, width), jnp.float32),
            pltpu.VMEM((3, width, model), jnp.bfloat16),
            pltpu.VMEM((3, rows, width), jnp.float32),
            pltpu.VMEM(piece, jnp.float32),
            pltpu.VMEM((2,) + piece, jnp.float32),
            pltpu.VMEM((2,) + piece, jnp.float32),
            pltpu.VMEM(piece, jnp.float32),
            pltpu.VMEM(piece, jnp.float32),
            pltpu.SemaphoreType.DMA((4, n_seq)),
            pltpu.SemaphoreType.DMA((4, n_seq)),
            pltpu.SemaphoreType.DMA((4, n_seq)),
            pltpu.SemaphoreType.DMA((3,)),
            pltpu.SemaphoreType.DMA((3,)),
            pltpu.SemaphoreType.DMA((3,)),
        ],
        compiler_params=pltpu.CompilerParams(collective_id=0, has_side_effects=True),
    )(queries, keys, values, out_grad, w_query, w_key, w_value)


def solution(mesh):
    placed = (
        P("seq", "head"),
        P("seq", "head"),
        P("seq", "head"),
        P("seq", "head"),
        P("head", None),
        P("head", None),
        P("head", None),
    )
    n_seq, n_head = mesh.shape["seq"], mesh.shape["head"]

    def per_device(queries, *rest):
        rows = queries.shape[0]
        rounds = (n_seq - 1).bit_length()
        direct = (n_seq - 1) * rows < rounds * (HD * (HD + 1) // 2)
        if direct and n_seq % 2 == 0 and n_head == 4:
            return direct_form(n_seq, n_head, queries, *rest)
        return on_device(queries, *rest)

    return jax.shard_map(
        per_device, mesh=mesh, in_specs=placed, out_specs=P("seq", "head"), check_vma=False
    )
```

```python
import functools

import jax
import jax.numpy as jnp
import numpy as np
from jax import lax
from jax.experimental import pallas as pl
from jax.experimental.pallas import tpu as pltpu
from jax.sharding import PartitionSpec as P

HD = 64
MESH = pl.DeviceIdType.MESH


def shifted(value, axis, steps):
    count = lax.axis_size(axis)
    leading, last = (max(0, -steps), min(count, count - steps))
    return lax.ppermute(value, axis, [(source, source + steps) for source in range(leading, last)])


def pair_tables(width):
    first, second = np.triu_indices(width)
    count = first.shape[0]
    select_first = np.zeros((width, count), np.float32)
    select_second = np.zeros((width, count), np.float32)
    select_first[first, np.arange(count)] = 1.0
    select_second[second, np.arange(count)] = 1.0
    scaling = np.where(first == second, 1.0, np.sqrt(2.0)) / width
    return (select_first, select_second, scaling.astype(np.float32))


def expand_features(inputs, pick_first, pick_second, scaling):
    first = jnp.dot(inputs, pick_first, preferred_element_type=jnp.bfloat16)
    second = jnp.dot(inputs, pick_second, preferred_element_type=jnp.bfloat16)
    feats = (first.astype(jnp.float32) * second.astype(jnp.float32) * scaling).astype(jnp.bfloat16)
    return (first, second, feats)


def chain_back(first, second, dphi, back_first, back_second, scaling):
    scaled = dphi * scaling
    left = scaled * second.astype(jnp.float32)
    right = scaled * first.astype(jnp.float32)
    return jnp.dot(
        left, back_first, precision=lax.Precision.HIGHEST, preferred_element_type=jnp.float32
    ) + jnp.dot(
        right, back_second, precision=lax.Precision.HIGHEST, preferred_element_type=jnp.float32
    )


def on_device(queries, keys, values, out_grad, w_query, w_key, w_value):
    count_rows = queries.shape[0]
    head_count = queries.shape[1] // HD
    select_first, select_second, scale_np = pair_tables(HD)
    pick_first = jnp.asarray(select_first, jnp.bfloat16)
    pick_second = jnp.asarray(select_second, jnp.bfloat16)
    back_first = jnp.asarray(select_first.T, jnp.float32)
    back_second = jnp.asarray(select_second.T, jnp.float32)
    scaling = jnp.asarray(scale_np, jnp.float32)
    feat_count = scale_np.shape[0]
    query_heads = queries.reshape(count_rows, head_count, HD)
    key_heads = keys.reshape(count_rows, head_count, HD)
    value_heads = values.reshape(count_rows, head_count, HD)
    grad_heads = out_grad.reshape(count_rows, head_count, HD)
    query_expanded = []
    key_expanded = []
    kv_parts = []
    grad_parts = []
    for number in range(head_count):
        query_set = expand_features(query_heads[:, number], pick_first, pick_second, scaling)
        key_set = expand_features(key_heads[:, number], pick_first, pick_second, scaling)
        query_expanded.append(query_set)
        key_expanded.append(key_set)
        kv_parts.append(
            jnp.einsum(
                "tf,td->fd", key_set[2], value_heads[:, number], preferred_element_type=jnp.float32
            )
        )
        grad_parts.append(
            jnp.einsum(
                "tf,td->fd", query_set[2], grad_heads[:, number], preferred_element_type=jnp.float32
            )
        )
    kv_local = jnp.stack(kv_parts, 1).reshape(feat_count, head_count * HD)
    grad_local = jnp.stack(grad_parts, 1).reshape(feat_count, head_count * HD)
    rounds = (lax.axis_size("seq") - 1).bit_length()
    kv_running = kv_local
    grad_running = grad_local
    for level in range(rounds):
        kv_running = kv_running + shifted(kv_running, "seq", 1 << level)
        grad_running = grad_running + shifted(grad_running, "seq", -(1 << level))
    kv_before = kv_running - kv_local
    grad_after = grad_running - grad_local
    kv_before = kv_before.astype(jnp.bfloat16).reshape(feat_count, head_count, HD)
    grad_after = grad_after.astype(jnp.bfloat16).reshape(feat_count, head_count, HD)
    causal = lax.broadcasted_iota(jnp.int32, (count_rows, count_rows), 0) >= lax.broadcasted_iota(
        jnp.int32, (count_rows, count_rows), 1
    )
    scores = jnp.einsum("thd,shd->hts", query_heads, key_heads, preferred_element_type=jnp.float32)
    products = jnp.einsum(
        "thd,shd->hts", grad_heads, value_heads, preferred_element_type=jnp.float32
    )
    attn = jnp.where(causal, (scores / HD) ** 2, 0.0).astype(jnp.bfloat16)
    pgrad = jnp.where(causal, 2.0 * scores * products / (HD * HD), 0.0).astype(jnp.bfloat16)
    query_local = jnp.einsum("hts,shd->thd", pgrad, key_heads, preferred_element_type=jnp.float32)
    key_local = jnp.einsum("hts,thd->shd", pgrad, query_heads, preferred_element_type=jnp.float32)
    value_local = jnp.einsum("hts,thd->shd", attn, grad_heads, preferred_element_type=jnp.float32)
    query_out = []
    key_out = []
    value_out = []
    for number in range(head_count):
        qfirst, qsecond, query_feat = query_expanded[number]
        kfirst, ksecond, key_feat = key_expanded[number]
        dfq = jnp.einsum(
            "td,fd->tf",
            grad_heads[:, number],
            kv_before[:, number],
            preferred_element_type=jnp.float32,
        )
        dfk = jnp.einsum(
            "td,fd->tf",
            value_heads[:, number],
            grad_after[:, number],
            preferred_element_type=jnp.float32,
        )
        query_out.append(
            query_local[:, number]
            + chain_back(qfirst, qsecond, dfq, back_first, back_second, scaling)
        )
        key_out.append(
            key_local[:, number]
            + chain_back(kfirst, ksecond, dfk, back_first, back_second, scaling)
        )
        value_out.append(
            value_local[:, number]
            + jnp.einsum(
                "tf,fd->td", key_feat, grad_after[:, number], preferred_element_type=jnp.float32
            )
        )
    query_grad = jnp.stack(query_out, 1).astype(jnp.bfloat16).reshape(count_rows, head_count * HD)
    key_grad = jnp.stack(key_out, 1).astype(jnp.bfloat16).reshape(count_rows, head_count * HD)
    value_grad = jnp.stack(value_out, 1).astype(jnp.bfloat16).reshape(count_rows, head_count * HD)
    partial_sum = jnp.dot(query_grad, w_query, preferred_element_type=jnp.float32)
    partial_sum = partial_sum + jnp.dot(key_grad, w_key, preferred_element_type=jnp.float32)
    partial_sum = partial_sum + jnp.dot(value_grad, w_value, preferred_element_type=jnp.float32)
    return lax.psum_scatter(partial_sum, "head", scatter_dimension=1, tiled=True).astype(
        jnp.bfloat16
    )


def stacked(block):
    lanes = lax.broadcasted_iota(jnp.int32, block.shape, 1)
    low = jnp.where(lanes < HD, block, 0.0).astype(jnp.bfloat16)
    high = jnp.where(lanes >= HD, block, 0.0).astype(jnp.bfloat16)
    return jnp.concatenate([low, high], axis=0)


def rows_dot(left, right):
    return lax.dot_general(
        left, right, (((1,), (1,)), ((), ())), preferred_element_type=jnp.float32
    )


def direct_kernel(
    n_seq,
    q_hbm,
    k_hbm,
    v_hbm,
    g_hbm,
    wq_hbm,
    wk_hbm,
    wv_hbm,
    out,
    own,
    buffers,
    weights,
    totals,
    own_part,
    core_send,
    core_recv,
    far_send,
    far_recv,
    recv_sem,
    line_sem,
    side_sem,
    own_sem,
    weight_sem,
    reduce_send_sem,
    reduce_recv_sem,
):
    K, V, Q, G = range(4)
    unused, rows, width = own.shape
    pairs = width // (2 * HD)
    lines = n_seq // 2
    me = lax.axis_index("seq")
    line, side = me // 2, me % 2
    other = 2 * line + (1 - side)
    head = lax.axis_index("head")
    far, core = head // 2, head % 2
    core_mate = 2 * far + (1 - core)
    far_mate = 2 * (1 - far) + core
    out_width = out.shape[1]
    has_up = line < lines - 1
    has_down = line > 0
    lower, upper = 2 * line < lines, 2 * line >= lines

    own_copies = [
        pltpu.make_async_copy(source, own.at[i], own_sem.at[i])
        for i, source in enumerate((k_hbm, v_hbm, q_hbm, g_hbm))
    ]
    for copy in own_copies:
        copy.start()

    barrier = pltpu.get_barrier_semaphore()

    def greet(target):
        pl.semaphore_signal(barrier, inc=1, device_id=target, device_id_type=MESH)

    greet({"seq": other})
    greet({"head": core_mate})
    greet({"head": far_mate})

    @pl.when(has_up)
    def _():
        greet({"seq": me + 2})

    @pl.when(has_down)
    def _():
        greet({"seq": me - 2})

    weight_copies = [
        pltpu.make_async_copy(source, weights.at[i], weight_sem.at[i])
        for i, source in enumerate((wq_hbm, wk_hbm, wv_hbm))
    ]
    for copy in weight_copies:
        copy.start()
    for which, copy in enumerate(own_copies):
        copy.wait()
        for p in range(pairs):
            buffers[which, me, p] = own[which, :, 2 * HD * p : 2 * HD * (p + 1)].astype(
                jnp.float32
            )

    pl.semaphore_wait(barrier, 3 + has_up.astype(jnp.int32) + has_down.astype(jnp.int32))

    def transfer(which, block, p, sem, target):
        return pltpu.make_async_remote_copy(
            src_ref=buffers.at[which, block, p],
            dst_ref=buffers.at[which, block, p],
            send_sem=sem.at[which, block, p],
            recv_sem=recv_sem.at[which, block, p],
            device_id={"seq": target},
            device_id_type=MESH,
        )

    def along(which, block, p):
        return transfer(which, block, p, line_sem, me + 2 if which in (K, V) else me - 2)

    def across(which, block, p):
        return transfer(which, block, p, side_sem, other)

    def guarded(condition, body):
        if condition is True:
            body()
        elif condition is not False:
            pl.when(condition)(body)

    def act_on(copy, act):
        copy.start() if act == "start" else copy.wait_send()

    def visit(step, which, p, act, line_part, side_part):
        rising = which in (K, V)
        block = me - 2 * step if rising else me + 2 * step
        present = (line >= step) if rising else (line + step < lines)
        onward = has_up if rising else has_down
        if step == 0:
            crosses = side == (0 if rising else 1)
        elif step == 1 or which in (K, Q):
            crosses = True
        else:
            crosses = False if step == lines - 1 else jnp.logical_not(onward)

        def body():
            if line_part:
                if step and act == "start":
                    along(which, block, p).wait_recv()
                guarded(onward, lambda: act_on(along(which, block, p), act))
            if side_part:
                guarded(crosses, lambda: act_on(across(which, block, p), act))

        guarded(present if step else True, body)

    def own_column(step, act):
        def urgent(first, second):
            for now, later in zip(first, second):
                for p in range(pairs):
                    visit(step, now, p, act, True, True)
                    visit(step, later, p, act, True, False)
            for later in second:
                for p in range(pairs):
                    visit(step, later, p, act, False, True)

        if step == 1 and act == "start":
            pl.when(lower & has_down)(lambda: urgent((K, V), (Q, G)))
            pl.when(upper & has_up)(lambda: urgent((Q, G), (K, V)))

            @pl.when(jnp.logical_not(has_up & has_down))
            def _():
                for pair in ((K, Q), (V, G)):
                    for p in range(pairs):
                        for which in pair:
                            visit(step, which, p, act, True, True)
        else:
            for pair in ((K, Q), (V, G)):
                for p in range(pairs):
                    for which in pair:
                        visit(step, which, p, act, True, True)

    def other_column(step, act, which):
        rising = which in (K, V)
        block = other - 2 * step if rising else other + 2 * step
        if step == 0:
            present = side == (1 if rising else 0)
        else:
            present = (line >= step) if rising else (line + step < lines)
        onward = False
        if 1 <= step < lines - 1 and which in (V, G):
            onward = has_up if rising else has_down
            if step < lines - 2:
                onward = (line < lines - 2) if rising else (line > 1)

        def body():
            for p in range(pairs):
                if act == "start":
                    across(which, block, p).wait_recv()
                guarded(onward, lambda: act_on(along(which, block, p), act))

        guarded(present, body)

    def query_role(block, diagonal=False):
        for p in range(pairs):
            part = slice(2 * HD * p, 2 * HD * (p + 1))
            k2 = stacked(buffers[K, block, p])
            v2 = stacked(buffers[V, block, p])
            scores = rows_dot(own[Q, :, part], k2)
            products = rows_dot(own[G, :, part], v2)
            weight = scores * products * (2.0 / (HD * HD))
            if diagonal:
                t = lax.broadcasted_iota(jnp.int32, weight.shape, 0)
                s = lax.broadcasted_iota(jnp.int32, weight.shape, 1) % rows
                weight = jnp.where(t >= s, weight, 0.0)
            result = jnp.dot(
                weight.astype(jnp.bfloat16), k2, preferred_element_type=jnp.float32
            )
            if diagonal:
                totals[0, :, part] = result
            else:
                totals[0, :, part] += result

    def key_role(block, diagonal=False):
        for p in range(pairs):
            part = slice(2 * HD * p, 2 * HD * (p + 1))
            q2 = stacked(buffers[Q, block, p])
            g2 = stacked(buffers[G, block, p])
            scores = rows_dot(own[K, :, part], q2)
            products = rows_dot(own[V, :, part], g2)
            weight = scores * products * (2.0 / (HD * HD))
            attn = (scores * (1.0 / HD)) * (scores * (1.0 / HD))
            if diagonal:
                s = lax.broadcasted_iota(jnp.int32, weight.shape, 0)
                t = lax.broadcasted_iota(jnp.int32, weight.shape, 1) % rows
                weight = jnp.where(t >= s, weight, 0.0)
                attn = jnp.where(t >= s, attn, 0.0)
            key_result = jnp.dot(
                weight.astype(jnp.bfloat16), q2, preferred_element_type=jnp.float32
            )
            value_result = jnp.dot(
                attn.astype(jnp.bfloat16), g2, preferred_element_type=jnp.float32
            )
            if diagonal:
                totals[1, :, part] = key_result
                totals[2, :, part] = value_result
            else:
                totals[1, :, part] += key_result
                totals[2, :, part] += value_result

    def compute_query(step, origin):
        present = side == 1 if step == 0 else line >= step
        pl.when(present)(lambda: query_role(origin - 2 * step))

    def compute_key(step, origin):
        present = side == 0 if step == 0 else line + step < lines
        pl.when(present)(lambda: key_role(origin + 2 * step))

    def from_side(step, arrays):
        for which in arrays:
            other_column(step, "start", which)

    own_column(0, "start")
    query_role(me, diagonal=True)
    key_role(me, diagonal=True)
    for step in range(1, lines):
        own_column(step, "start")
        if step == 1:
            from_side(0, (V, G, K, Q))
        else:
            if step > 2:
                from_side(step - 1, (V, G))
            else:
                pl.when(lower)(lambda: from_side(1, (V, K)))
                pl.when(upper)(lambda: from_side(1, (G, Q)))
        compute_query(step, me)
        compute_key(step, me)
        if step == 1:
            compute_query(0, other)
            compute_key(0, other)
        elif step == 2:
            pl.when(lower)(lambda: compute_query(1, other))
            pl.when(upper)(lambda: compute_key(1, other))
        else:
            if step == 3:
                pl.when(lower)(lambda: from_side(1, (G, Q)))
                pl.when(upper)(lambda: from_side(1, (V, K)))
                pl.when(lower)(lambda: compute_key(1, other))
                pl.when(upper)(lambda: compute_query(1, other))
            from_side(step - 1, (K, Q))
            compute_query(step - 1, other)
            compute_key(step - 1, other)
    last = lines - 1
    if last <= 2:
        if last == 2:
            pl.when(lower)(lambda: from_side(1, (G, Q)))
            pl.when(upper)(lambda: from_side(1, (V, K)))
            pl.when(lower)(lambda: compute_key(1, other))
            pl.when(upper)(lambda: compute_query(1, other))
    if last:
        from_side(last, (K, Q, V, G))
        compute_query(last, other)
        compute_key(last, other)

    for copy in weight_copies:
        copy.wait()
    final = [totals[i].astype(jnp.bfloat16) for i in (0, 1, 2)]

    chunks = far_send.shape[0]
    chunk_width = out_width // chunks

    def project(target, first, count):
        start = target * out_width + first
        cols = pl.ds(pl.multiple_of(start, chunk_width), count)
        return sum(
            jnp.dot(final[i], weights[i, :, cols], preferred_element_type=jnp.float32)
            for i in range(3)
        )

    def to_core(slot):
        return pltpu.make_async_remote_copy(
            src_ref=core_send.at[slot],
            dst_ref=core_recv.at[slot],
            send_sem=reduce_send_sem.at[slot],
            recv_sem=reduce_recv_sem.at[slot],
            device_id={"head": core_mate},
            device_id_type=MESH,
        )

    def to_far(i):
        return pltpu.make_async_remote_copy(
            src_ref=far_send.at[i],
            dst_ref=far_recv.at[i],
            send_sem=reduce_send_sem.at[2 * chunks + i],
            recv_sem=reduce_recv_sem.at[2 * chunks + i],
            device_id={"head": far_mate},
            device_id_type=MESH,
        )

    def pass_far(i):
        to_core(i).wait_recv()
        far_send[i] += core_recv[i]
        to_far(i).start()

    for i in range(chunks):
        core_send[i] = project(2 * (1 - far) + (1 - core), i * chunk_width, chunk_width)
        to_core(i).start()
        far_send[i] = project(far_mate, i * chunk_width, chunk_width)
        if i:
            pass_far(i - 1)
    pass_far(chunks - 1)
    for i in range(chunks):
        core_send[chunks + i] = project(core_mate, i * chunk_width, chunk_width)
        to_core(chunks + i).start()
    own_part[...] = project(head, 0, out_width)
    for i in range(chunks):
        part = slice(i * chunk_width, (i + 1) * chunk_width)
        to_core(chunks + i).wait_recv()
        own_part[:, part] += core_recv[chunks + i]
    for i in range(chunks):
        part = slice(i * chunk_width, (i + 1) * chunk_width)
        to_far(i).wait_recv()
        out[:, part] = (own_part[:, part] + far_recv[i]).astype(out.dtype)

    for i in range(2 * chunks):
        to_core(i).wait_send()
    for i in range(chunks):
        to_far(i).wait_send()
    for step in range(lines):
        own_column(step, "finish")
        for which in (K, V, Q, G):
            other_column(step, "finish", which)


def direct_form(n_seq, n_head, queries, keys, values, out_grad, w_query, w_key, w_value):
    rows, width = queries.shape
    model = w_query.shape[1]
    out_width = model // n_head
    pairs = width // (2 * HD)
    chunks = 1
    piece = (rows, out_width // chunks)
    return pl.pallas_call(
        functools.partial(direct_kernel, n_seq),
        out_shape=jax.ShapeDtypeStruct((rows, out_width), jnp.bfloat16),
        in_specs=[pl.BlockSpec(memory_space=pl.ANY)] * 7,
        out_specs=pl.BlockSpec(memory_space=pltpu.VMEM),
        scratch_shapes=[
            pltpu.VMEM((4, rows, width), jnp.bfloat16),
            pltpu.VMEM((4, n_seq, pairs, rows, 2 * HD), jnp.float32),
            pltpu.VMEM((3, width, model), jnp.bfloat16),
            pltpu.VMEM((3, rows, width), jnp.float32),
            pltpu.VMEM((rows, out_width), jnp.float32),
            pltpu.VMEM((2 * chunks,) + piece, jnp.float32),
            pltpu.VMEM((2 * chunks,) + piece, jnp.float32),
            pltpu.VMEM((chunks,) + piece, jnp.float32),
            pltpu.VMEM((chunks,) + piece, jnp.float32),
            pltpu.SemaphoreType.DMA((4, n_seq, pairs)),
            pltpu.SemaphoreType.DMA((4, n_seq, pairs)),
            pltpu.SemaphoreType.DMA((4, n_seq, pairs)),
            pltpu.SemaphoreType.DMA((4,)),
            pltpu.SemaphoreType.DMA((3,)),
            pltpu.SemaphoreType.DMA((3 * chunks,)),
            pltpu.SemaphoreType.DMA((3 * chunks,)),
        ],
        compiler_params=pltpu.CompilerParams(collective_id=0, has_side_effects=True),
    )(queries, keys, values, out_grad, w_query, w_key, w_value)


def solution(mesh):
    placed = (
        P("seq", "head"),
        P("seq", "head"),
        P("seq", "head"),
        P("seq", "head"),
        P("head", None),
        P("head", None),
        P("head", None),
    )
    n_seq, n_head = mesh.shape["seq"], mesh.shape["head"]

    def per_device(queries, *rest):
        rows = queries.shape[0]
        rounds = (n_seq - 1).bit_length()
        direct = (n_seq - 1) * rows < rounds * (HD * (HD + 1) // 2)
        if direct and n_seq % 2 == 0 and n_head == 4:
            return direct_form(n_seq, n_head, queries, *rest)
        return on_device(queries, *rest)

    return jax.shard_map(
        per_device, mesh=mesh, in_specs=placed, out_specs=P("seq", "head"), check_vma=False
    )
```

```python
import functools

import jax
import jax.numpy as jnp
import numpy as np
from jax import lax
from jax.experimental import pallas as pl
from jax.experimental.pallas import tpu as pltpu
from jax.sharding import PartitionSpec as P

HD = 64
MESH = pl.DeviceIdType.MESH


def shifted(value, axis, steps):
    count = lax.axis_size(axis)
    leading, last = (max(0, -steps), min(count, count - steps))
    return lax.ppermute(value, axis, [(source, source + steps) for source in range(leading, last)])


def pair_tables(width):
    first, second = np.triu_indices(width)
    count = first.shape[0]
    select_first = np.zeros((width, count), np.float32)
    select_second = np.zeros((width, count), np.float32)
    select_first[first, np.arange(count)] = 1.0
    select_second[second, np.arange(count)] = 1.0
    scaling = np.where(first == second, 1.0, np.sqrt(2.0)) / width
    return (select_first, select_second, scaling.astype(np.float32))


def expand_features(inputs, pick_first, pick_second, scaling):
    first = jnp.dot(inputs, pick_first, preferred_element_type=jnp.bfloat16)
    second = jnp.dot(inputs, pick_second, preferred_element_type=jnp.bfloat16)
    feats = (first.astype(jnp.float32) * second.astype(jnp.float32) * scaling).astype(jnp.bfloat16)
    return (first, second, feats)


def chain_back(first, second, dphi, back_first, back_second, scaling):
    scaled = dphi * scaling
    left = scaled * second.astype(jnp.float32)
    right = scaled * first.astype(jnp.float32)
    return jnp.dot(
        left, back_first, precision=lax.Precision.HIGHEST, preferred_element_type=jnp.float32
    ) + jnp.dot(
        right, back_second, precision=lax.Precision.HIGHEST, preferred_element_type=jnp.float32
    )


def on_device(queries, keys, values, out_grad, w_query, w_key, w_value):
    count_rows = queries.shape[0]
    head_count = queries.shape[1] // HD
    select_first, select_second, scale_np = pair_tables(HD)
    pick_first = jnp.asarray(select_first, jnp.bfloat16)
    pick_second = jnp.asarray(select_second, jnp.bfloat16)
    back_first = jnp.asarray(select_first.T, jnp.float32)
    back_second = jnp.asarray(select_second.T, jnp.float32)
    scaling = jnp.asarray(scale_np, jnp.float32)
    feat_count = scale_np.shape[0]
    query_heads = queries.reshape(count_rows, head_count, HD)
    key_heads = keys.reshape(count_rows, head_count, HD)
    value_heads = values.reshape(count_rows, head_count, HD)
    grad_heads = out_grad.reshape(count_rows, head_count, HD)
    query_expanded = []
    key_expanded = []
    kv_parts = []
    grad_parts = []
    for number in range(head_count):
        query_set = expand_features(query_heads[:, number], pick_first, pick_second, scaling)
        key_set = expand_features(key_heads[:, number], pick_first, pick_second, scaling)
        query_expanded.append(query_set)
        key_expanded.append(key_set)
        kv_parts.append(
            jnp.einsum(
                "tf,td->fd", key_set[2], value_heads[:, number], preferred_element_type=jnp.float32
            )
        )
        grad_parts.append(
            jnp.einsum(
                "tf,td->fd", query_set[2], grad_heads[:, number], preferred_element_type=jnp.float32
            )
        )
    kv_local = jnp.stack(kv_parts, 1).reshape(feat_count, head_count * HD)
    grad_local = jnp.stack(grad_parts, 1).reshape(feat_count, head_count * HD)
    rounds = (lax.axis_size("seq") - 1).bit_length()
    kv_running = kv_local
    grad_running = grad_local
    for level in range(rounds):
        kv_running = kv_running + shifted(kv_running, "seq", 1 << level)
        grad_running = grad_running + shifted(grad_running, "seq", -(1 << level))
    kv_before = kv_running - kv_local
    grad_after = grad_running - grad_local
    kv_before = kv_before.astype(jnp.bfloat16).reshape(feat_count, head_count, HD)
    grad_after = grad_after.astype(jnp.bfloat16).reshape(feat_count, head_count, HD)
    causal = lax.broadcasted_iota(jnp.int32, (count_rows, count_rows), 0) >= lax.broadcasted_iota(
        jnp.int32, (count_rows, count_rows), 1
    )
    scores = jnp.einsum("thd,shd->hts", query_heads, key_heads, preferred_element_type=jnp.float32)
    products = jnp.einsum(
        "thd,shd->hts", grad_heads, value_heads, preferred_element_type=jnp.float32
    )
    attn = jnp.where(causal, (scores / HD) ** 2, 0.0).astype(jnp.bfloat16)
    pgrad = jnp.where(causal, 2.0 * scores * products / (HD * HD), 0.0).astype(jnp.bfloat16)
    query_local = jnp.einsum("hts,shd->thd", pgrad, key_heads, preferred_element_type=jnp.float32)
    key_local = jnp.einsum("hts,thd->shd", pgrad, query_heads, preferred_element_type=jnp.float32)
    value_local = jnp.einsum("hts,thd->shd", attn, grad_heads, preferred_element_type=jnp.float32)
    query_out = []
    key_out = []
    value_out = []
    for number in range(head_count):
        qfirst, qsecond, query_feat = query_expanded[number]
        kfirst, ksecond, key_feat = key_expanded[number]
        dfq = jnp.einsum(
            "td,fd->tf",
            grad_heads[:, number],
            kv_before[:, number],
            preferred_element_type=jnp.float32,
        )
        dfk = jnp.einsum(
            "td,fd->tf",
            value_heads[:, number],
            grad_after[:, number],
            preferred_element_type=jnp.float32,
        )
        query_out.append(
            query_local[:, number]
            + chain_back(qfirst, qsecond, dfq, back_first, back_second, scaling)
        )
        key_out.append(
            key_local[:, number]
            + chain_back(kfirst, ksecond, dfk, back_first, back_second, scaling)
        )
        value_out.append(
            value_local[:, number]
            + jnp.einsum(
                "tf,fd->td", key_feat, grad_after[:, number], preferred_element_type=jnp.float32
            )
        )
    query_grad = jnp.stack(query_out, 1).astype(jnp.bfloat16).reshape(count_rows, head_count * HD)
    key_grad = jnp.stack(key_out, 1).astype(jnp.bfloat16).reshape(count_rows, head_count * HD)
    value_grad = jnp.stack(value_out, 1).astype(jnp.bfloat16).reshape(count_rows, head_count * HD)
    partial_sum = jnp.dot(query_grad, w_query, preferred_element_type=jnp.float32)
    partial_sum = partial_sum + jnp.dot(key_grad, w_key, preferred_element_type=jnp.float32)
    partial_sum = partial_sum + jnp.dot(value_grad, w_value, preferred_element_type=jnp.float32)
    return lax.psum_scatter(partial_sum, "head", scatter_dimension=1, tiled=True).astype(
        jnp.bfloat16
    )


def stacked(block):
    lanes = lax.broadcasted_iota(jnp.int32, block.shape, 1)
    low = jnp.where(lanes < HD, block, 0.0).astype(jnp.bfloat16)
    high = jnp.where(lanes >= HD, block, 0.0).astype(jnp.bfloat16)
    return jnp.concatenate([low, high], axis=0)


def rows_dot(left, right):
    return lax.dot_general(
        left, right, (((1,), (1,)), ((), ())), preferred_element_type=jnp.float32
    )


def direct_kernel(
    n_seq,
    q_hbm,
    k_hbm,
    v_hbm,
    g_hbm,
    wq_hbm,
    wk_hbm,
    wv_hbm,
    out,
    own,
    buffers,
    weights,
    totals,
    own_part,
    core_send,
    core_recv,
    far_send,
    far_recv,
    recv_sem,
    line_sem,
    side_sem,
    own_sem,
    weight_sem,
    reduce_send_sem,
    reduce_recv_sem,
):
    K, V, Q, G = range(4)
    unused, rows, width = own.shape
    pairs = width // (2 * HD)
    lines = n_seq // 2
    me = lax.axis_index("seq")
    line, side = me // 2, me % 2
    other = 2 * line + (1 - side)
    head = lax.axis_index("head")
    far, core = head // 2, head % 2
    core_mate = 2 * far + (1 - core)
    far_mate = 2 * (1 - far) + core
    out_width = out.shape[1]
    has_up = line < lines - 1
    has_down = line > 0
    lower, upper = 2 * line < lines, 2 * line >= lines

    barrier = pltpu.get_barrier_semaphore()

    def greet(target):
        pl.semaphore_signal(barrier, inc=1, device_id=target, device_id_type=MESH)

    greet({"seq": other})
    greet({"head": core_mate})
    greet({"head": far_mate})

    @pl.when(has_up)
    def _():
        greet({"seq": me + 2})

    @pl.when(has_down)
    def _():
        greet({"seq": me - 2})

    own_copies = [
        pltpu.make_async_copy(source, own.at[i], own_sem.at[i])
        for i, source in enumerate((k_hbm, v_hbm, q_hbm, g_hbm))
    ]
    for copy in own_copies:
        copy.start()

    weight_copies = [
        pltpu.make_async_copy(source, weights.at[i], weight_sem.at[i])
        for i, source in enumerate((wq_hbm, wk_hbm, wv_hbm))
    ]
    for copy in weight_copies:
        copy.start()
    for which, copy in enumerate(own_copies):
        copy.wait()
        for p in range(pairs):
            buffers[which, me, p] = own[which, :, 2 * HD * p : 2 * HD * (p + 1)].astype(
                jnp.float32
            )

    pl.semaphore_wait(barrier, 3 + has_up.astype(jnp.int32) + has_down.astype(jnp.int32))

    def transfer(which, block, p, sem, target):
        return pltpu.make_async_remote_copy(
            src_ref=buffers.at[which, block, p],
            dst_ref=buffers.at[which, block, p],
            send_sem=sem.at[which, block, p],
            recv_sem=recv_sem.at[which, block, p],
            device_id={"seq": target},
            device_id_type=MESH,
        )

    def along(which, block, p):
        return transfer(which, block, p, line_sem, me + 2 if which in (K, V) else me - 2)

    def across(which, block, p):
        return transfer(which, block, p, side_sem, other)

    def guarded(condition, body):
        if condition is True:
            body()
        elif condition is not False:
            pl.when(condition)(body)

    def act_on(copy, act):
        copy.start() if act == "start" else copy.wait_send()

    def visit(step, which, p, act, line_part, side_part):
        rising = which in (K, V)
        block = me - 2 * step if rising else me + 2 * step
        present = (line >= step) if rising else (line + step < lines)
        onward = has_up if rising else has_down
        if step == 0:
            crosses = side == (0 if rising else 1)
        elif step == 1 or which in (K, Q):
            crosses = True
        else:
            crosses = False if step == lines - 1 else jnp.logical_not(onward)

        def body():
            if line_part:
                if step and act == "start":
                    along(which, block, p).wait_recv()
                guarded(onward, lambda: act_on(along(which, block, p), act))
            if side_part:
                guarded(crosses, lambda: act_on(across(which, block, p), act))

        guarded(present if step else True, body)

    def own_column(step, act):
        def urgent(first, second):
            for now, later in zip(first, second):
                for p in range(pairs):
                    visit(step, now, p, act, True, True)
                    visit(step, later, p, act, True, False)
            for later in second:
                for p in range(pairs):
                    visit(step, later, p, act, False, True)

        if step == 1 and act == "start":
            pl.when(lower & has_down)(lambda: urgent((K, V), (Q, G)))
            pl.when(upper & has_up)(lambda: urgent((Q, G), (K, V)))

            @pl.when(jnp.logical_not(has_up & has_down))
            def _():
                for pair in ((K, Q), (V, G)):
                    for p in range(pairs):
                        for which in pair:
                            visit(step, which, p, act, True, True)
        else:
            for pair in ((K, Q), (V, G)):
                for p in range(pairs):
                    for which in pair:
                        visit(step, which, p, act, True, True)

    def other_column(step, act, which):
        rising = which in (K, V)
        block = other - 2 * step if rising else other + 2 * step
        if step == 0:
            present = side == (1 if rising else 0)
        else:
            present = (line >= step) if rising else (line + step < lines)
        onward = False
        if 1 <= step < lines - 1 and which in (V, G):
            onward = has_up if rising else has_down
            if step < lines - 2:
                onward = (line < lines - 2) if rising else (line > 1)

        def body():
            for p in range(pairs):
                if act == "start":
                    across(which, block, p).wait_recv()
                guarded(onward, lambda: act_on(along(which, block, p), act))

        guarded(present, body)

    def query_role(block, diagonal=False):
        for p in range(pairs):
            part = slice(2 * HD * p, 2 * HD * (p + 1))
            k2 = stacked(buffers[K, block, p])
            v2 = stacked(buffers[V, block, p])
            scores = rows_dot(own[Q, :, part], k2)
            products = rows_dot(own[G, :, part], v2)
            weight = scores * products * (2.0 / (HD * HD))
            if diagonal:
                t = lax.broadcasted_iota(jnp.int32, weight.shape, 0)
                s = lax.broadcasted_iota(jnp.int32, weight.shape, 1) % rows
                weight = jnp.where(t >= s, weight, 0.0)
            result = jnp.dot(
                weight.astype(jnp.bfloat16), k2, preferred_element_type=jnp.float32
            )
            if diagonal:
                totals[0, :, part] = result
            else:
                totals[0, :, part] += result

    def key_role(block, diagonal=False):
        for p in range(pairs):
            part = slice(2 * HD * p, 2 * HD * (p + 1))
            q2 = stacked(buffers[Q, block, p])
            g2 = stacked(buffers[G, block, p])
            scores = rows_dot(own[K, :, part], q2)
            products = rows_dot(own[V, :, part], g2)
            weight = scores * products * (2.0 / (HD * HD))
            attn = (scores * (1.0 / HD)) * (scores * (1.0 / HD))
            if diagonal:
                s = lax.broadcasted_iota(jnp.int32, weight.shape, 0)
                t = lax.broadcasted_iota(jnp.int32, weight.shape, 1) % rows
                weight = jnp.where(t >= s, weight, 0.0)
                attn = jnp.where(t >= s, attn, 0.0)
            key_result = jnp.dot(
                weight.astype(jnp.bfloat16), q2, preferred_element_type=jnp.float32
            )
            value_result = jnp.dot(
                attn.astype(jnp.bfloat16), g2, preferred_element_type=jnp.float32
            )
            if diagonal:
                totals[1, :, part] = key_result
                totals[2, :, part] = value_result
            else:
                totals[1, :, part] += key_result
                totals[2, :, part] += value_result

    def compute_query(step, origin):
        present = side == 1 if step == 0 else line >= step
        pl.when(present)(lambda: query_role(origin - 2 * step))

    def compute_key(step, origin):
        present = side == 0 if step == 0 else line + step < lines
        pl.when(present)(lambda: key_role(origin + 2 * step))

    def from_side(step, arrays):
        for which in arrays:
            other_column(step, "start", which)

    own_column(0, "start")
    query_role(me, diagonal=True)
    key_role(me, diagonal=True)
    for step in range(1, lines):
        own_column(step, "start")
        if step == 1:
            from_side(0, (V, G, K, Q))
        else:
            if step > 2:
                from_side(step - 1, (V, G))
            else:
                pl.when(lower)(lambda: from_side(1, (V, K)))
                pl.when(upper)(lambda: from_side(1, (G, Q)))
        compute_query(step, me)
        compute_key(step, me)
        if step == 1:
            compute_query(0, other)
            compute_key(0, other)
        elif step == 2:
            pl.when(lower)(lambda: compute_query(1, other))
            pl.when(upper)(lambda: compute_key(1, other))
        else:
            if step == 3:
                pl.when(lower)(lambda: from_side(1, (G, Q)))
                pl.when(upper)(lambda: from_side(1, (V, K)))
                pl.when(lower)(lambda: compute_key(1, other))
                pl.when(upper)(lambda: compute_query(1, other))
            from_side(step - 1, (K, Q))
            compute_query(step - 1, other)
            compute_key(step - 1, other)
    last = lines - 1
    if last <= 2:
        if last == 2:
            pl.when(lower)(lambda: from_side(1, (G, Q)))
            pl.when(upper)(lambda: from_side(1, (V, K)))
            pl.when(lower)(lambda: compute_key(1, other))
            pl.when(upper)(lambda: compute_query(1, other))
    if last:
        from_side(last, (K, Q, V, G))
        compute_query(last, other)
        compute_key(last, other)

    for copy in weight_copies:
        copy.wait()
    final = [totals[i].astype(jnp.bfloat16) for i in (0, 1, 2)]

    chunks = far_send.shape[0]
    chunk_width = out_width // chunks

    def project(target, first, count):
        start = target * out_width + first
        cols = pl.ds(pl.multiple_of(start, chunk_width), count)
        return sum(
            jnp.dot(final[i], weights[i, :, cols], preferred_element_type=jnp.float32)
            for i in range(3)
        )

    def to_core(slot):
        return pltpu.make_async_remote_copy(
            src_ref=core_send.at[slot],
            dst_ref=core_recv.at[slot],
            send_sem=reduce_send_sem.at[slot],
            recv_sem=reduce_recv_sem.at[slot],
            device_id={"head": core_mate},
            device_id_type=MESH,
        )

    def to_far(i):
        return pltpu.make_async_remote_copy(
            src_ref=far_send.at[i],
            dst_ref=far_recv.at[i],
            send_sem=reduce_send_sem.at[2 * chunks + i],
            recv_sem=reduce_recv_sem.at[2 * chunks + i],
            device_id={"head": far_mate},
            device_id_type=MESH,
        )

    def pass_far(i):
        to_core(i).wait_recv()
        far_send[i] += core_recv[i]
        to_far(i).start()

    for i in range(chunks):
        core_send[i] = project(2 * (1 - far) + (1 - core), i * chunk_width, chunk_width)
        to_core(i).start()
        far_send[i] = project(far_mate, i * chunk_width, chunk_width)
        if i:
            pass_far(i - 1)
    pass_far(chunks - 1)
    for i in range(chunks):
        core_send[chunks + i] = project(core_mate, i * chunk_width, chunk_width)
        to_core(chunks + i).start()
    own_part[...] = project(head, 0, out_width)
    for i in range(chunks):
        part = slice(i * chunk_width, (i + 1) * chunk_width)
        to_core(chunks + i).wait_recv()
        own_part[:, part] += core_recv[chunks + i]
    for i in range(chunks):
        part = slice(i * chunk_width, (i + 1) * chunk_width)
        to_far(i).wait_recv()
        out[:, part] = (own_part[:, part] + far_recv[i]).astype(out.dtype)

    for i in range(2 * chunks):
        to_core(i).wait_send()
    for i in range(chunks):
        to_far(i).wait_send()
    for step in range(lines):
        own_column(step, "finish")
        for which in (K, V, Q, G):
            other_column(step, "finish", which)


def direct_form(n_seq, n_head, queries, keys, values, out_grad, w_query, w_key, w_value):
    rows, width = queries.shape
    model = w_query.shape[1]
    out_width = model // n_head
    pairs = width // (2 * HD)
    chunks = 1
    piece = (rows, out_width // chunks)
    return pl.pallas_call(
        functools.partial(direct_kernel, n_seq),
        out_shape=jax.ShapeDtypeStruct((rows, out_width), jnp.bfloat16),
        in_specs=[pl.BlockSpec(memory_space=pl.ANY)] * 7,
        out_specs=pl.BlockSpec(memory_space=pltpu.VMEM),
        scratch_shapes=[
            pltpu.VMEM((4, rows, width), jnp.bfloat16),
            pltpu.VMEM((4, n_seq, pairs, rows, 2 * HD), jnp.float32),
            pltpu.VMEM((3, width, model), jnp.bfloat16),
            pltpu.VMEM((3, rows, width), jnp.float32),
            pltpu.VMEM((rows, out_width), jnp.float32),
            pltpu.VMEM((2 * chunks,) + piece, jnp.float32),
            pltpu.VMEM((2 * chunks,) + piece, jnp.float32),
            pltpu.VMEM((chunks,) + piece, jnp.float32),
            pltpu.VMEM((chunks,) + piece, jnp.float32),
            pltpu.SemaphoreType.DMA((4, n_seq, pairs)),
            pltpu.SemaphoreType.DMA((4, n_seq, pairs)),
            pltpu.SemaphoreType.DMA((4, n_seq, pairs)),
            pltpu.SemaphoreType.DMA((4,)),
            pltpu.SemaphoreType.DMA((3,)),
            pltpu.SemaphoreType.DMA((3 * chunks,)),
            pltpu.SemaphoreType.DMA((3 * chunks,)),
        ],
        compiler_params=pltpu.CompilerParams(collective_id=0, has_side_effects=True),
    )(queries, keys, values, out_grad, w_query, w_key, w_value)


def solution(mesh):
    placed = (
        P("seq", "head"),
        P("seq", "head"),
        P("seq", "head"),
        P("seq", "head"),
        P("head", None),
        P("head", None),
        P("head", None),
    )
    n_seq, n_head = mesh.shape["seq"], mesh.shape["head"]

    def per_device(queries, *rest):
        rows = queries.shape[0]
        rounds = (n_seq - 1).bit_length()
        direct = (n_seq - 1) * rows < rounds * (HD * (HD + 1) // 2)
        if direct and n_seq % 2 == 0 and n_head == 4:
            return direct_form(n_seq, n_head, queries, *rest)
        return on_device(queries, *rest)

    return jax.shard_map(
        per_device, mesh=mesh, in_specs=placed, out_specs=P("seq", "head"), check_vma=False
    )
```
